32 devices in a mesh: dp: 8 (over y, x, core), mp: 4 (over z).
Axes of the slice: x: 2, y: 2, z: 4, core: 2. Of those that a mesh axis runs over, the one named last changes fastest.
Arguments:
- tokens: bfloat16 [16384, 1024], P(('dp', 'mp')), may hold values from -6 to 6
- cotangent: bfloat16 [16384, 1024], P(('dp', 'mp')), may hold values from -6 to 6
- seq_len: int32 [8, 8], P('dp'), may hold values from 0 to 2048, as said below
- gain_attn: float32 [1024], replicated, may hold values from 0.1 to 1.9
- w_query: bfloat16 [1024, 256], P(None, 'mp'), may hold values from -0.1875 to 0.1875
- w_key: bfloat16 [1024, 256], P(None, 'mp'), may hold values from -0.1875 to 0.1875
- w_value: bfloat16 [1024, 1024], P(None, 'mp'), may hold values from -0.1875 to 0.1875
- w_out: bfloat16 [1024, 1024], P('mp'), may hold values from -1 to 1
- gain_ffn: float32 [1024], replicated, may hold values from 0.1 to 1.9
- w_gate: bfloat16 [1024, 2752], P(None, 'mp'), may hold values from -0.1875 to 0.1875
- w_up: bfloat16 [1024, 2752], P(None, 'mp'), may hold values from -0.1875 to 0.1875
- w_down: bfloat16 [2752, 1024], P('mp'), may hold values from -0.109375 to 0.109375
Outputs:
- mixed: bfloat16 [16384, 1024], P(('dp', 'mp'))
- grad_tokens: float32 [16384, 1024], P(('dp', 'mp'))
- grad_gain_attn: float32 [1024], replicated
- grad_w_query: float32 [1024, 256], P(None, 'mp')
- grad_w_key: float32 [1024, 256], P(None, 'mp')
- grad_w_value: float32 [1024, 1024], P(None, 'mp')
- grad_w_out: float32 [1024, 1024], P('mp')
- grad_gain_ffn: float32 [1024], replicated
- grad_w_gate: float32 [1024, 2752], P(None, 'mp')
- grad_w_up: float32 [1024, 2752], P(None, 'mp')
- grad_w_down: float32 [2752, 1024], P('mp')
The draws below stay inside these ranges and needn't reach their ends.
Inputs may be any that keep to these rules, and one draw needn't show every extreme that they name: `seq_len`: the nonzero lengths of a row come first and sum to 2048; each is 256, 1024 or 2048; some row holds one sequence of 2048 tokens and some row holds 8 sequences of 256.
All inputs are finite; a program needn't handle non-finite values.
Results may differ from the reference program's by a relative error of at most 0.017.
Values may be sent and summed in bfloat16 or wider, within the bound.
No kernel may reach another device: no remote copies, remote signals or barrier semaphores. Data moves between devices by JAX's collectives and lax.ppermute only.
A program may use at most 192 MiB of HBM per device.

```python
import jax
import jax.numpy as jnp
import numpy as np
from jax import lax

D = 1024
HEADS = 16
FEAT = 16
HEAD_V = 64
FF = 2752
BLOCK = 512
TAYLOR = 273
TOK_GROUP = 2048
GROUPS = 8
TOKENS = 16384


length_patterns = np.array([[8, 0, 0, 0, 0, 0, 0, 0], [4, 4, 0, 0, 0, 0, 0, 0], [4, 1, 1, 1, 1, 0, 0, 0], [1, 4, 1, 1, 1, 0, 0, 0], [1, 1, 4, 1, 1, 0, 0, 0], [1, 1, 1, 4, 1, 0, 0, 0], [1, 1, 1, 1, 4, 0, 0, 0], [1, 1, 1, 1, 1, 1, 1, 1]], dtype=np.int32)


def draw_seq_len(key, part):
    key_pick, key_first, key_second = jax.random.split(key, 3)
    picks = jax.random.randint(key_pick, (GROUPS,), 0, 8)
    first = jax.random.randint(key_first, (), 0, GROUPS)
    second = (first + jax.random.randint(key_second, (), 1, GROUPS)) % GROUPS
    places = jnp.arange(GROUPS)
    picks = jnp.where(places == first, 0, picks)
    picks = jnp.where(places == second, 7, picks)
    table = jnp.asarray(length_patterns)
    return (table[picks] * (TOK_GROUP // 8)).astype(jnp.int32)


def shard_levels(stream_key, shape, cuts, low, high):
    level = 1.0
    for dim, parts in cuts:
        steps = jax.random.uniform(jax.random.fold_in(jax.random.fold_in(stream_key, 6), dim), (parts,), jnp.float32, low / len(cuts), high / len(cuts))
        level = level * jnp.repeat(jnp.exp(steps), shape[dim] // parts).reshape((-1,) + (1,) * (len(shape) - 1 - dim))
    return level


def noise(own_key, extent, spread, bound, cuts=(), kind=jnp.bfloat16):
    drawn = jax.random.normal(own_key, extent, jnp.float32) * spread
    if len(cuts) > 0:
        drawn = shard_levels(own_key, extent, cuts, -0.22, 0.18) * drawn
    return jnp.clip(drawn, min=-bound, max=bound).astype(kind)


def setup_inputs(seed: int = 0) -> dict:
    key_list = jax.random.split(jax.random.key(seed), 13)
    tokens = noise(key_list[0], (TOKENS, D), 1.0, 6.0, ((0, 32),))
    cotangent = noise(key_list[1], (TOKENS, D), 1.0, 6.0, ((0, 32),))
    seq_len = draw_seq_len(jax.random.fold_in(key_list[12], 71), 0)
    gain_attn = jnp.clip(1.0 + 0.18 * jax.random.normal(key_list[3], (D,), jnp.float32), 0.1, 1.9)
    w_query = noise(key_list[4], (D, HEADS * FEAT), D ** -0.5, 0.1875, ((1, 4),))
    w_key = noise(key_list[5], (D, HEADS * FEAT), D ** -0.5, 0.1875, ((1, 4),))
    w_value = noise(key_list[6], (D, HEADS * HEAD_V), D ** -0.5, 0.1875, ((1, 4),))
    w_out = noise(key_list[7], (HEADS * HEAD_V, D), (D // 32) ** -0.5, 1.0, ((0, 4),))
    gain_ffn = jnp.clip(1.0 + 0.18 * jax.random.normal(key_list[8], (D,), jnp.float32), 0.1, 1.9)
    w_gate = noise(key_list[9], (D, FF), D ** -0.5, 0.1875, ((1, 4),))
    w_up = noise(key_list[10], (D, FF), D ** -0.5, 0.1875, ((1, 4),))
    w_down = noise(key_list[11], (FF, D), FF ** -0.5, 0.109375, ((0, 4),))
    return dict(tokens=tokens, cotangent=cotangent, seq_len=seq_len, gain_attn=gain_attn, w_query=w_query, w_key=w_key, w_value=w_value, w_out=w_out, gain_ffn=gain_ffn, w_gate=w_gate, w_up=w_up, w_down=w_down)


EPSILON = 1e-05
HIGHEST = lax.Precision.HIGHEST

@jax.custom_vjp
def low(v):
    return lax.optimization_barrier(v.astype(jnp.bfloat16)).astype(jnp.float32)

@jax.custom_vjp
def low_back(v):
    return v

def low_keep(v):
    return (low(v), None)

def low_pass(kept, grad):
    return (grad,)

def back_keep(v):
    return (v, None)

def back_low(kept, grad):
    return (low(grad),)
low.defvjp(low_keep, low_pass)
low_back.defvjp(back_keep, back_low)

def matmul(left, right):
    return jnp.dot(left, right, precision=HIGHEST, preferred_element_type=jnp.float32)

def features(values):
    squares = (values[..., :, None] * values[..., None, :]).reshape(values.shape[:-1] + (FEAT * FEAT,))
    constant = jnp.ones(values.shape[:-1] + (1,), jnp.float32)
    return jnp.concatenate([constant, values * FEAT ** (-0.25), squares * (2.0 * FEAT) ** (-0.5)], axis=-1)

def sequence_ids(lengths, places_count):
    starts = (jnp.cumsum(lengths) - lengths).astype(jnp.int32)
    places = jnp.arange(places_count, dtype=jnp.int32)
    started = (starts[None, :] <= places[:, None]) & (lengths[None, :] > 0)
    return lax.optimization_barrier(jnp.sum(started.astype(jnp.int32), axis=1)).astype(jnp.int32) - 1

def block_masks(seg_ids, block_rows):
    seg_blocks = seg_ids.reshape(-1, block_rows)
    before = jnp.concatenate([jnp.full((1,), -1, jnp.int32), seg_blocks[:-1, -1]])
    carry_in = (seg_blocks == before[:, None]).astype(jnp.float32)
    key_keep = (seg_blocks == seg_blocks[:, -1:]).astype(jnp.float32)
    passing = carry_in[:, -1]
    causal = jnp.arange(block_rows)[:, None] >= jnp.arange(block_rows)[None, :]
    same_seq = ((seg_blocks[:, :, None] == seg_blocks[:, None, :]) & causal[None]).astype(jnp.float32)
    return (carry_in, key_keep, passing, same_seq)

def attend_block(carried, blocked):
    states, totals = carried
    query_rows, key_rows, value_rows, carry_in, key_keep, passing, same_seq = blocked
    product = low_back(jnp.einsum('ihf,jhf->hij', query_rows, key_rows, precision=HIGHEST))
    scores = product * FEAT ** (-0.5)
    kernel = (1.0 + scores + 0.5 * scores * scores) * same_seq[None]
    numerator = low_back(jnp.einsum('hij,jhv->ihv', low(kernel), value_rows, precision=HIGHEST))
    query_feat = features(query_rows) * carry_in[:, None, None]
    numerator = numerator + jnp.einsum('ihf,hfv->ihv', query_feat, states, precision=HIGHEST)
    denominator = lax.optimization_barrier(jnp.sum(kernel, axis=2)).T + jnp.einsum('ihf,hf->ih', query_feat, totals, precision=HIGHEST)
    attended = numerator / denominator[:, :, None]
    key_feat = features(key_rows) * key_keep[:, None, None]
    new_states = passing * states + jnp.einsum('jhf,jhv->hfv', key_feat, value_rows, precision=HIGHEST)
    new_totals = passing * totals + lax.optimization_barrier(jnp.sum(key_feat, axis=0))
    return ((new_states, new_totals), attended)

def layer(inputs, gain_attn, w_query, w_key, w_value, w_out, gain_ffn, w_gate, w_up, w_down, masks):
    carry_in, key_keep, passing, same_seq = masks
    group_rows = inputs.shape[0]
    block_count = group_rows // BLOCK
    root_attn = lax.rsqrt(lax.optimization_barrier(jnp.mean(inputs * inputs, axis=1, keepdims=True)) + EPSILON)
    normed_attn = low(inputs * root_attn * gain_attn)
    query_rows = low(low_back(matmul(normed_attn, w_query))).reshape(block_count, BLOCK, HEADS, FEAT)
    key_rows = low(low_back(matmul(normed_attn, w_key))).reshape(block_count, BLOCK, HEADS, FEAT)
    value_rows = low(low_back(matmul(normed_attn, w_value))).reshape(block_count, BLOCK, HEADS, HEAD_V)
    zero_states = jnp.zeros((HEADS, TAYLOR, HEAD_V), jnp.float32)
    zero_totals = jnp.zeros((HEADS, TAYLOR), jnp.float32)
    final_carry, attended = lax.scan(jax.checkpoint(attend_block), (zero_states, zero_totals), (query_rows, key_rows, value_rows, carry_in, key_keep, passing, same_seq))
    attn_low = low(attended.reshape(group_rows, HEADS * HEAD_V))
    hidden = inputs + low_back(matmul(attn_low, w_out))
    root_ffn = lax.rsqrt(lax.optimization_barrier(jnp.mean(hidden * hidden, axis=1, keepdims=True)) + EPSILON)
    normed_ffn = low(hidden * root_ffn * gain_ffn)
    gate_pre = low_back(matmul(normed_ffn, w_gate))
    up_pre = low_back(matmul(normed_ffn, w_up))
    activated = low(jax.nn.silu(gate_pre) * up_pre)
    return hidden + low_back(matmul(activated, w_down))

def reference(tokens, cotangent, seq_len, gain_attn, w_query, w_key, w_value, w_out, gain_ffn, w_gate, w_up, w_down):
    weights = tuple((weight.astype(jnp.float32) for weight in (gain_attn, w_query, w_key, w_value, w_out, gain_ffn, w_gate, w_up, w_down)))
    group_inputs = tokens.reshape(GROUPS, TOK_GROUP, D)
    group_grads = cotangent.reshape(GROUPS, TOK_GROUP, D)

    def one_group(totals_sofar, data):
        rows_in, rows_grad, lengths = data
        masks = block_masks(sequence_ids(lengths, TOK_GROUP), BLOCK)

        def forward(inputs, *params):
            return layer(inputs, *params, masks)
        outputs, pullback = jax.vjp(forward, rows_in.astype(jnp.float32), *weights)
        grads = pullback(rows_grad.astype(jnp.float32))
        new_totals = tuple((total + grad for total, grad in zip(totals_sofar, grads[1:])))
        return (new_totals, (outputs.astype(jnp.bfloat16), grads[0]))
    initial = tuple((jnp.zeros_like(weight) for weight in weights))
    sums, stacked = lax.scan(one_group, initial, (group_inputs, group_grads, seq_len))
    mixed = stacked[0].reshape(TOKENS, D)
    grad_tokens = stacked[1].reshape(TOKENS, D)
    return (mixed, grad_tokens, sums[0], sums[1], sums[2], sums[3], sums[4], sums[5], sums[6], sums[7], sums[8])
```

```python
import functools

import jax
import jax.numpy as jnp
from jax import lax
from jax.sharding import PartitionSpec as P

FEAT = 16
HEAD_V = 64
SHIFTS = FEAT // 2 + 1
EPSILON = 1e-05
BF16 = jnp.bfloat16
F32 = jnp.float32


def contract(left, right, left_dim, right_dim):
    return lax.dot_general(
        left, right, (((left_dim,), (right_dim,)), ((), ())), preferred_element_type=F32
    )


def hop(values, dp_size, bit):
    return lax.ppermute(values, "dp", [(i, i ^ (1 << bit)) for i in range(dp_size)])


def ring(values, mp_size, step=1):
    return lax.ppermute(values, "mp", [(i, (i + step) % mp_size) for i in range(mp_size)])


def pick(blocks, index):
    bit = 0
    while (1 << bit) < len(blocks):
        chosen = (index >> bit) & 1 == 1
        blocks = [
            jnp.where(chosen, blocks[r ^ (1 << bit)], blocks[r]) for r in range(len(blocks))
        ]
        bit += 1
    return blocks


def columns(values, parts):
    width = values.shape[1] // parts
    return [values[:, r * width : (r + 1) * width] for r in range(parts)]


def reorder(values, parts, index):
    return jnp.concatenate(pick(columns(values, parts), index), axis=1)


def half_of(values, core):
    middle = values.shape[0] // 2
    return jnp.where(core == 0, values[:middle], values[middle:])


def gather_plane(piece, dp_size):
    parts = dp_size // 2
    middle = piece.shape[0] // 2
    upper, lower = {0: piece[:middle]}, {0: piece[middle:]}
    whole = {0: piece}
    for r in sorted(range(1, parts), key=lambda r: (bin(r).count("1"), r)):
        high = r.bit_length() - 1
        low = (r & -r).bit_length() - 1
        if high == low:
            whole[r] = hop(piece, dp_size, high + 1)
            upper[r], lower[r] = whole[r][:middle], whole[r][middle:]
        else:
            upper[r] = hop(upper[r ^ (1 << high)], dp_size, high + 1)
            lower[r] = hop(lower[r ^ (1 << low)], dp_size, low + 1)
            whole[r] = jnp.concatenate([upper[r], lower[r]], axis=0)
    return [whole[r] for r in range(parts)]


def scatter_plane(blocks, dp_size):
    parts = dp_size // 2
    middle = blocks[0].shape[0] // 2
    upper = [[block[:middle]] for block in blocks]
    lower = [[block[middle:]] for block in blocks]

    def total(terms):
        if len(terms) == 1:
            return terms[0]
        return sum(term.astype(F32) for term in terms).astype(BF16)

    for r in sorted(range(1, parts), key=lambda r: (-bin(r).count("1"), r)):
        high = r.bit_length() - 1
        low = (r & -r).bit_length() - 1
        upper[r ^ (1 << high)].append(hop(total(upper[r]), dp_size, high + 1))
        lower[r ^ (1 << low)].append(hop(total(lower[r]), dp_size, low + 1))
    return jnp.concatenate([total(upper[0]), total(lower[0])], axis=0)


def scatter_ring(values, mp_size):
    slots = jnp.split(values, mp_size, axis=0)
    moving = slots[1 % mp_size]
    for slot in range(2, mp_size + 1):
        arrived = ring(moving, mp_size).astype(F32)
        moving = (arrived + slots[slot % mp_size].astype(F32)).astype(BF16)
    return moving


def gather_ring(piece, mp_size):
    slots = [piece]
    for _ in range(mp_size - 1):
        slots.append(ring(slots[-1], mp_size))
    return slots


def total_over_all(values, dp_size, mp_size):
    for bit in range(dp_size.bit_length() - 1):
        values = values + hop(values, dp_size, bit)
    for bit in range(mp_size.bit_length() - 1):
        pairs = [(i, i ^ (1 << bit)) for i in range(mp_size)]
        values = values + lax.ppermute(values, "mp", pairs)
    return values


def gather_weights(own, dp_size, mp_size):
    parts = dp_size // 2
    width = own.shape[1] // parts
    slots = gather_ring(own[:, :width], mp_size)
    pieces = gather_plane(jnp.concatenate(slots[1:], axis=0), dp_size)
    return jnp.concatenate([own, jnp.concatenate(pieces, axis=1)], axis=0)


def reduce_weights(blocks, dp_size, mp_size):
    return scatter_ring(scatter_plane(blocks, dp_size), mp_size)


def features(entries):
    quads = [
        entries
        * jnp.roll(entries, -d, axis=-2)
        * ((2.0 * FEAT) ** (-0.5) if d in (0, SHIFTS - 1) else FEAT ** (-0.5))
        for d in range(SHIFTS)
    ]
    constant = jnp.ones(entries.shape[:-2] + (1, entries.shape[-1]), F32)
    return jnp.concatenate(quads + [entries * FEAT ** (-0.25), constant], axis=-2)


def features_back(entries, grads):
    total = grads[..., SHIFTS * FEAT : (SHIFTS + 1) * FEAT, :] * FEAT ** (-0.25)
    for d in range(SHIFTS):
        weight = (2.0 * FEAT) ** (-0.5) if d in (0, SHIFTS - 1) else FEAT ** (-0.5)
        part = grads[..., d * FEAT : (d + 1) * FEAT, :] * weight
        total = total + part * jnp.roll(entries, -d, axis=-2)
        total = total + jnp.roll(part * entries, d, axis=-2)
    return total


def einsum(spec, left, right):
    return jnp.einsum(spec, left, right, preferred_element_type=F32)


def split_heads(joined, heads):
    query = joined[:, : heads * FEAT]
    key = joined[:, heads * FEAT : 2 * heads * FEAT]
    value = joined[:, 2 * heads * FEAT :]

    def shaped(values, size):
        slots, _, tokens = values.shape
        return values.reshape(slots, heads, size, 2, tokens // 2).transpose(0, 1, 3, 2, 4)

    return shaped(query, FEAT), shaped(key, FEAT), shaped(value, HEAD_V)


def merge_heads(values):
    slots, heads, groups, size, tokens = values.shape
    return values.transpose(0, 1, 3, 2, 4).reshape(slots, heads * size, groups * tokens)


def block_states(entries, values, extra, keep):
    feats = (features(entries.astype(F32)) * keep[:, None, :]).astype(BF16)
    states = einsum("shgfj,shgvj->shgfv", feats, values.astype(BF16))
    totals = einsum("shgfj,shgj->shgf", feats, extra.astype(BF16))
    return states, totals


def kernel_of(query, key, same):
    scores = einsum("shgfj,shgfi->shgji", key, query) * FEAT ** (-0.5)
    return scores, (1.0 + scores + 0.5 * scores * scores) * same


def attend(query, key, value, same, carry_in, states, totals):
    scores, kernel = kernel_of(query, key, same)
    num = einsum("shgvj,shgji->shgvi", value, kernel.astype(BF16))
    feats = (features(query.astype(F32)) * carry_in[:, None, :]).astype(BF16)
    num = num + einsum("shgfv,shgfi->shgvi", states.astype(BF16), feats)
    den = jnp.sum(kernel, axis=-2) + einsum("shgf,shgfi->shgi", totals.astype(BF16), feats)
    return num / den[..., None, :], den


def attend_back(query, key, value, same, carry_in, keep, states, totals, grads, d_num, d_den):
    grad_states, grad_totals = grads
    d_num_low = d_num.astype(BF16)
    scores, kernel = kernel_of(query, key, same)
    d_kernel = einsum("shgvj,shgvi->shgji", value, d_num_low) + d_den[..., None, :]
    d_prod = (d_kernel * same * (1.0 + scores) * FEAT ** (-0.5)).astype(BF16)
    d_query = einsum("shgfj,shgji->shgfi", key, d_prod)
    d_key = einsum("shgfi,shgji->shgfj", query, d_prod)
    d_value = einsum("shgvi,shgji->shgvj", d_num_low, kernel.astype(BF16))
    query32, key32 = query.astype(F32), key.astype(F32)
    d_qfeat = einsum("shgfv,shgvi->shgfi", states.astype(BF16), d_num_low)
    d_qfeat = (d_qfeat + totals[..., None] * d_den[..., None, :]) * carry_in[:, None, :]
    d_kfeat = einsum("shgfv,shgvj->shgfj", grad_states.astype(BF16), value)
    d_kfeat = (d_kfeat + grad_totals[..., None]) * keep[:, None, :]
    key_feat = (features(key32) * keep[:, None, :]).astype(BF16)
    d_value = d_value + einsum("shgfv,shgfj->shgvj", grad_states.astype(BF16), key_feat)
    d_query = d_query + features_back(query32, d_qfeat)
    d_key = d_key + features_back(key32, d_kfeat)
    return jnp.concatenate(
        [merge_heads(d_query), merge_heads(d_key), merge_heads(d_value)], axis=1
    ).astype(BF16)


def exchange(pair, coefs, mp_size, step):
    moving = [part.astype(BF16) for part in pair]
    sums = [0.0, 0.0]
    for distance in range(1, mp_size):
        moving = [ring(part, mp_size, step) for part in moving]
        weight = coefs[distance - 1]
        here = [jnp.roll(part, distance * step, axis=0).astype(F32) for part in moving]
        sums = [
            sums[0] + here[0] * weight[:, None, None],
            sums[1] + here[1] * weight[:, None],
        ]
    return sums


def norm_back(d_normed, unit_rows, root_rows, gain):
    scaled = d_normed * gain
    gain_part = jnp.sum(d_normed * unit_rows, axis=0, keepdims=True)
    d_rows = root_rows * (scaled - unit_rows * jnp.mean(scaled * unit_rows, axis=1, keepdims=True))
    return (d_rows, gain_part)


def padded(values, rows):
    return jnp.pad(values, ((0, rows - values.shape[0]), (0, 0)))


def shards(
    dp_size,
    mp_size,
    tokens,
    cotangent,
    seq_len,
    gain_attn,
    w_query,
    w_key,
    w_value,
    w_out,
    gain_ffn,
    w_gate,
    w_up,
    w_down,
):
    rows = tokens.shape[0]
    parts = dp_size // 2
    place = lax.axis_index("dp")
    core, plane = place & 1, place >> 1
    block = lax.axis_index("mp")
    heads = w_out.shape[0] // HEAD_V // 2
    units = w_gate.shape[1] // 2
    padded_units = -(-units // 16) * 16
    pair = functools.partial(hop, dp_size=dp_size, bit=0)
    relative = functools.partial(reorder, parts=parts, index=plane)

    own_attn = relative(
        jnp.concatenate([half_of(w.T, core) for w in (w_query, w_key, w_value)] + [half_of(w_out, core)], axis=0)
    )
    own_gate_up = relative(
        jnp.concatenate(
            [padded(half_of(w.T, core), padded_units) for w in (w_gate, w_up)], axis=0
        )
    )
    own_down = relative(padded(half_of(w_down, core), padded_units))
    attn_rows = own_attn.shape[0] - heads * HEAD_V
    all_attn = gather_weights(own_attn, dp_size, mp_size).reshape(mp_size, -1, own_attn.shape[1])
    all_joined = all_attn[:, :attn_rows].reshape(mp_size * attn_rows, -1)
    all_out = all_attn[:, attn_rows:].reshape(mp_size * heads * HEAD_V, -1)
    all_gate_up = gather_weights(own_gate_up, dp_size, mp_size)
    all_down = gather_weights(own_down, dp_size, mp_size)

    lengths = jnp.concatenate([seq_len, pair(seq_len)], axis=0)
    starts = jnp.cumsum(lengths, axis=1) - lengths

    def seq_at(places):
        started = (starts[:, None, :] <= places[None, :, None]) & (lengths[:, None, :] > 0)
        return jnp.sum(started.astype(jnp.int32), axis=2) - 1

    seq = seq_at(block * rows + jnp.arange(rows))
    last = seq_at((block + jnp.arange(-mp_size, mp_size + 1)) * rows + rows - 1)
    before = jnp.where(block > 0, last[:, mp_size - 1], -1)
    carry_in = (seq == before[:, None]).astype(F32)
    keep = (seq == last[:, mp_size][:, None]).astype(F32)
    order = jnp.arange(rows)
    same = ((seq[:, :, None] == seq[:, None, :]) & (order[:, None] <= order[None, :])).astype(F32)
    ahead = [
        ((block >= t) & (last[:, mp_size - t] == last[:, mp_size - 1])).astype(F32)
        for t in range(1, mp_size)
    ]
    behind = [
        ((block + t < mp_size) & (last[:, mp_size + t - 1] == last[:, mp_size])).astype(F32)
        for t in range(1, mp_size)
    ]

    gain1 = relative(gain_attn[None, :])
    gain2 = relative(gain_ffn[None, :])
    inputs = relative(tokens).astype(F32)
    cot = relative(cotangent)
    cot_all = jnp.concatenate([cot, pair(cot)], axis=0)
    root1 = lax.rsqrt(jnp.mean(inputs * inputs, axis=1, keepdims=True) + EPSILON)
    unit1 = inputs * root1
    normed1 = (unit1 * gain1).astype(BF16)
    normed1_all = jnp.concatenate([normed1, pair(normed1)], axis=0)
    joined = contract(all_joined, normed1_all, 1, 1).astype(BF16)
    query, key, value = split_heads(joined.reshape(mp_size, attn_rows, 2 * rows), heads)
    ones = jnp.ones(value.shape[:3] + value.shape[4:], BF16)
    own_states = block_states(key, value, ones, keep)
    states, totals = exchange(own_states, ahead, mp_size, 1)
    attended, den = attend(query, key, value, same, carry_in, states, totals)
    attn_low = merge_heads(attended).astype(BF16).reshape(-1, 2 * rows)

    def pair_sum(product):
        other = pair(product(slice(rows, 2 * rows)).astype(BF16))
        return product(slice(0, rows)) + other.astype(F32)

    hidden = inputs + pair_sum(lambda part: contract(attn_low[:, part], all_out, 0, 0))

    root2 = lax.rsqrt(jnp.mean(hidden * hidden, axis=1, keepdims=True) + EPSILON)
    unit2 = hidden * root2
    normed2 = (unit2 * gain2).astype(BF16)
    normed2_all = jnp.concatenate([normed2, pair(normed2)], axis=0)
    gate_up = contract(all_gate_up, normed2_all, 1, 1).reshape(
        mp_size, 2, padded_units, 2 * rows
    )
    gate, up = gate_up[:, 0], gate_up[:, 1]
    d_act = contract(all_down, cot_all, 1, 1).reshape(mp_size, padded_units, 2 * rows)
    sigmoid = jax.nn.sigmoid(gate)
    silu = gate * sigmoid
    act = (silu * up).astype(BF16).reshape(-1, 2 * rows)
    d_gate = d_act * up * sigmoid * (1.0 + gate * (1.0 - sigmoid))
    d_up = d_act * silu
    d_gate_up = jnp.stack([d_gate, d_up], axis=1).astype(BF16).reshape(-1, 2 * rows)
    mixed = hidden + pair_sum(lambda part: contract(act[:, part], all_down, 0, 0))
    d_normed2 = pair_sum(lambda part: contract(d_gate_up[:, part], all_gate_up, 0, 0))

    def grads_of(left, right):
        return [contract(left, block, 1, 0).astype(BF16) for block in columns(right, parts)]

    reduce = functools.partial(reduce_weights, dp_size=dp_size, mp_size=mp_size)
    piece_down = reduce(grads_of(act, cot_all))
    piece_gate_up = reduce(grads_of(d_gate_up, normed2_all))

    d_rows2, gain2_part = norm_back(d_normed2, unit2, root2, gain2)
    d_hidden = cot.astype(F32) + d_rows2
    d_attn = d_hidden.astype(BF16)
    d_attn_all = jnp.concatenate([d_attn, pair(d_attn)], axis=0)

    d_out = contract(all_out, d_attn_all, 1, 0 + 1).reshape(mp_size, heads, HEAD_V, 2, rows)
    d_out = d_out.transpose(0, 1, 3, 2, 4)
    piece_out = reduce(grads_of(attn_low, d_attn_all))
    d_num = d_out / den[..., None, :]
    d_den = -jnp.sum(d_out * attended, axis=-2) / den
    own_grads = block_states(query, d_num, d_den, carry_in)
    grads = exchange(own_grads, behind, mp_size, -1)
    d_joined = attend_back(
        query, key, value, same, carry_in, keep, states, totals, grads, d_num, d_den
    ).reshape(-1, 2 * rows)
    piece_joined = reduce(grads_of(d_joined, normed1_all))
    d_normed1 = pair_sum(lambda part: contract(d_joined[:, part], all_joined, 0, 0))
    d_rows1, gain1_part = norm_back(d_normed1, unit1, root1, gain1)
    grad_tokens = d_hidden + d_rows1
    gains = total_over_all(
        relative(jnp.concatenate([gain1_part, gain2_part], axis=0)), dp_size, mp_size
    )

    def whole(piece):
        blocks = gather_plane(piece, dp_size)
        others = [pair(block) for block in blocks]
        lower = [jnp.where(core == 0, a, b) for a, b in zip(blocks, others)]
        upper = [jnp.where(core == 0, b, a) for a, b in zip(blocks, others)]
        return pick(lower, plane), pick(upper, plane)

    def unit_columns(piece, first, count):
        lower, upper = piece
        return jnp.concatenate(
            [
                jnp.concatenate([a[:, first : first + count], b[:, first : first + count]], axis=1)
                for a, b in zip(lower, upper)
            ],
            axis=0,
        ).astype(F32)

    def unit_rows(piece, count):
        lower, upper = piece
        return jnp.concatenate(
            [
                jnp.concatenate([a[:count] for a in lower], axis=1),
                jnp.concatenate([b[:count] for b in upper], axis=1),
            ],
            axis=0,
        ).astype(F32)

    whole_gate_up = whole(piece_gate_up.T)
    whole_joined = whole(piece_joined.T)
    size = heads * FEAT
    return (
        relative(mixed.astype(BF16)),
        relative(grad_tokens),
        gains[0],
        unit_columns(whole_joined, 0, size),
        unit_columns(whole_joined, size, size),
        unit_columns(whole_joined, 2 * size, heads * HEAD_V),
        unit_rows(whole(piece_out), heads * HEAD_V),
        gains[1],
        unit_columns(whole_gate_up, 0, units),
        unit_columns(whole_gate_up, padded_units, units),
        unit_rows(whole(piece_down), units),
    )


def solution(mesh):
    body = functools.partial(shards, mesh.shape["dp"], mesh.shape["mp"])
    tokens = P(("dp", "mp"), None)
    out_columns, in_rows = P(None, "mp"), P("mp", None)
    return jax.shard_map(
        body,
        mesh=mesh,
        in_specs=(
            tokens, tokens, P("dp", None), P(), out_columns, out_columns, out_columns, in_rows,
            P(), out_columns, out_columns, in_rows,
        ),
        out_specs=(
            tokens, tokens, P(), out_columns, out_columns, out_columns, in_rows, P(),
            out_columns, out_columns, in_rows,
        ),
        check_vma=False,
    )
```
